32 devices in a mesh: nodes: 8 (over z, x), feat: 4 (over y, core).
Axes of the slice: x: 2, y: 2, z: 4, core: 2. Of those that a mesh axis runs over, the one named last changes fastest.
Arguments:
- features: bfloat16 [128, 32768], P('feat', 'nodes'), may hold values from -6 to 6
- w_self: bfloat16 [128, 256], replicated, may hold values from -0.5 to 0.5
- w_neigh: bfloat16 [128, 256], replicated, may hold values from -0.5 to 0.5
- hidden_bias: float32 [256], replicated, may hold values from -3 to 3
- cotangent: bfloat16 [256, 32768], P('feat', 'nodes'), may hold values from -0.032958984 to 0.032958984
- hub_local: int32 [8, 32], P('nodes'), may hold values from 0 to 4095
- send_rows: int32 [8, 8, 128], P('nodes'), may hold values from 0 to 4095
- send_count: int32 [8, 8], P('nodes'), may hold values from 0 to 128, as said below
- tile_values: bfloat16 [1024, 128, 128], P('nodes'), may hold values from 0 to 0.039794922
- tile_target: int32 [8, 128], P('nodes'), may hold values from 0 to 31, as said below
- tile_anchor: int32 [8, 128], P('nodes'), may hold values from 0 to 41, as said below
- tile_count: int32 [8], P('nodes'), may hold values from 42 to 128, as said below
Outputs:
- hidden: bfloat16 [256, 32768], P('feat', 'nodes')
- grad_self: float32 [128, 256], P(None, 'feat')
- grad_neigh: float32 [128, 256], P(None, 'feat')
- bias_grad: float32 [256], P('feat')
The draws below stay inside these ranges and needn't reach their ends.
Inputs may be any that keep to these rules, and one draw needn't show every extreme that they name: hub_local[q, j] is the local row of partition q's j-th hub node; hubs are ordered by owner, then by j. send_rows[q, p, j] is the local row of partition q that fills slot j of what q sends to p; slots at or after send_count[q, p] are padding. `send_count`: A partition sends nothing to itself, and every partition fills all 128 slots for at least one other partition. `tile_target`: A block is 128 consecutive local nodes. On every partition each block is the destination of some live tile. `tile_anchor`: A block is 128 consecutive rows of source_p. On every partition each source block that holds halo or hub rows is used by some live tile. Tile slots at or after tile_count[p] are padding: their tile_values, tile_target and tile_anchor entries are arbitrary and must be ignored. Some partition fills all 128 slots.
All inputs are finite; a program needn't handle non-finite values.
Results may differ from the reference program's by a relative error of at most 0.0055.
Values may be sent and summed in bfloat16 or wider, within the bound.
No kernel may reach another device: no remote copies, remote signals or barrier semaphores. Data moves between devices by JAX's collectives and lax.ppermute only.
A program may use at most 64 MiB of HBM per device.

```python
import jax
import jax.numpy as jnp
from jax import lax

F_IN = 128
HID = 256
NP = 4096
SLOT = 128
HUB_DEV = 32
TB = 128
NODES = 32768
SOURCE = 5376
BASE_TILES = 42
TILES = 128
N_NODES = 8


def tile_layout(key):
    keys = jax.random.split(jax.random.fold_in(key, 41), 6)
    local_blocks = NP // TB
    source_blocks = SOURCE // TB
    spare = TILES - BASE_TILES
    first_target = jnp.broadcast_to(jnp.arange(local_blocks, dtype=jnp.int32)[None, :], (N_NODES, local_blocks))
    other_target = jax.random.randint(keys[0], (N_NODES, BASE_TILES - local_blocks), 0, local_blocks, dtype=jnp.int32)
    spare_target = jax.random.randint(keys[1], (N_NODES, spare), 0, local_blocks, dtype=jnp.int32)
    targets = jnp.concatenate([first_target, other_target, spare_target], axis=1)
    first_anchor = jax.random.randint(keys[2], (N_NODES, local_blocks), 0, local_blocks, dtype=jnp.int32)
    other_anchor = jnp.broadcast_to(jnp.arange(local_blocks, source_blocks, dtype=jnp.int32)[None, :], (N_NODES, source_blocks - local_blocks))
    spare_anchor = jax.random.randint(keys[3], (N_NODES, spare), 0, source_blocks, dtype=jnp.int32)
    anchors = jnp.concatenate([first_anchor, other_anchor, spare_anchor], axis=1)
    level = jax.random.randint(keys[4], (N_NODES,), 0, 1001, dtype=jnp.int32)
    chosen = jax.random.randint(keys[5], (), 0, N_NODES, dtype=jnp.int32)
    level = jnp.where(jnp.arange(N_NODES, dtype=jnp.int32) == chosen, 1000, level)
    cubed = level * level // 1000 * level // 1000
    counts = BASE_TILES + spare * cubed // 1000
    return (targets, anchors, counts.astype(jnp.int32))


def draw_tile_target(key, part):
    return tile_layout(key)[0]


def draw_tile_anchor(key, part):
    return tile_layout(key)[1]


def draw_tile_count(key, part):
    return tile_layout(key)[2]


def draw_send_count(key, part):
    counts = jax.random.randint(jax.random.fold_in(key, 17), (N_NODES, N_NODES), SLOT // 4, SLOT + 1, dtype=jnp.int32)
    senders = lax.broadcasted_iota(jnp.int32, (N_NODES, N_NODES), 0)
    takers = lax.broadcasted_iota(jnp.int32, (N_NODES, N_NODES), 1)
    counts = jnp.where(takers == (senders + 1) % N_NODES, SLOT, counts)
    counts = jnp.where(senders == takers, 0, counts)
    return counts


def set_ends(drawn, stream_key, smallest, top_value):
    shape = drawn.shape
    spot = [jax.random.randint(jax.random.fold_in(stream_key, axis), (), 0, shape[axis]) for axis in range(len(shape))]
    drawn = drawn.at[tuple(spot)].set(smallest)
    longest = shape.index(max(shape))
    spot[longest] = (spot[longest] + 1) % shape[longest]
    return drawn.at[tuple(spot)].set(top_value)


def shard_levels(rng, dims, pieces, low, top_value):
    gain, own = 1.0, jax.random.fold_in(rng, 6)
    for axis_at, shards_of in pieces:
        steps = jnp.exp(jax.random.uniform(jax.random.fold_in(own, axis_at), (shards_of,), jnp.float32, low / len(pieces), top_value / len(pieces)))
        gain = gain * jnp.repeat(steps, dims[axis_at] // shards_of).reshape([-1 if axis == axis_at else 1 for axis in range(len(dims))])
    return gain


def centred(rng, dims, width, most, cuts=(), kind=jnp.bfloat16):
    loudness = shard_levels(rng, dims, cuts, -0.22, 0.18) if cuts else 1.0
    values = jax.random.normal(rng, dims, jnp.float32) * width * loudness
    return jnp.minimum(jnp.maximum(values, -most), most).astype(kind)


def setup_inputs(seed: int = 0) -> dict:
    splits = jax.random.split(jax.random.key(seed), 13)
    return {
        "features": centred(splits[0], (F_IN, NODES), 1.0, 6.0, ((0, 4), (1, 8))),
        "w_self": centred(splits[1], (F_IN, HID), F_IN ** -0.5, 0.5),
        "w_neigh": centred(splits[2], (F_IN, HID), F_IN ** -0.5, 0.5),
        "hidden_bias": centred(splits[3], (HID,), 0.5, 3.0, (), jnp.float32),
        "cotangent": centred(splits[4], (HID, NODES), (1.0 / NODES ** 0.5), 0.032958984, ((0, 4), (1, 8))),
        "hub_local": set_ends(jax.random.randint(splits[5], (N_NODES, HUB_DEV), 0, NP), jax.random.fold_in(splits[5], 1), 0, NP - 1).astype(jnp.int32),
        "send_rows": set_ends(jax.random.randint(splits[6], (N_NODES, N_NODES, SLOT), 0, NP), jax.random.fold_in(splits[6], 1), 0, NP - 1).astype(jnp.int32),
        "send_count": draw_send_count(jax.random.fold_in(splits[12], 71), 0),
        "tile_values": jnp.clip(0.039794922 * jax.random.uniform(splits[8], (N_NODES * TILES, TB, TB), jnp.float32) ** shard_levels(splits[8], (N_NODES * TILES, TB, TB), ((0, 8),), -0.2, 0.2), 0.0, 0.039794922).astype(jnp.bfloat16),
        "tile_target": draw_tile_target(jax.random.fold_in(splits[12], 71), 0),
        "tile_anchor": draw_tile_anchor(jax.random.fold_in(splits[12], 71), 0),
        "tile_count": draw_tile_count(jax.random.fold_in(splits[12], 71), 0),
    }


def reference(features, w_self, w_neigh, hidden_bias, cotangent, hub_local, send_rows, send_count, tile_values, tile_target, tile_anchor, tile_count):
    owner_base = jnp.arange(N_NODES, dtype=jnp.int32)[:, None] * NP
    hub_index = (owner_base + hub_local).reshape(-1).astype(jnp.int32)
    hub_rows = jnp.take(features, hub_index, axis=1)
    slot_index = lax.broadcasted_iota(jnp.int32, (N_NODES, SLOT), 1)
    local_blocks = NP // TB
    block_ids = jnp.arange(local_blocks, dtype=jnp.int32)

    def one_part(part_index):
        own_rows = lax.dynamic_slice_in_dim(features, (part_index * NP).astype(jnp.int32), NP, 1)
        sent_rows = jnp.take(send_rows, part_index, axis=1)
        live_slot = slot_index < jnp.take(send_count, part_index, axis=1)[:, None]
        halo_rows = jnp.take(features, (owner_base + sent_rows).reshape(-1).astype(jnp.int32), axis=1)
        halo_rows = jnp.where(live_slot.reshape(1, -1), halo_rows, jnp.zeros_like(halo_rows))
        source_rows = jnp.concatenate([own_rows, halo_rows, hub_rows], axis=1).reshape(F_IN, SOURCE // TB, TB)
        tile_block = lax.dynamic_slice_in_dim(tile_values, (part_index * TILES).astype(jnp.int32), TILES, 0).astype(jnp.float32)
        targets = jnp.take(tile_target, part_index, axis=0)
        anchors = jnp.take(tile_anchor, part_index, axis=0)
        live_tiles = jnp.arange(TILES, dtype=jnp.int32) < jnp.take(tile_count, part_index)
        picked = jnp.take(source_rows, anchors, axis=1).astype(jnp.float32)
        products = jnp.einsum("ftk,tik->fti", picked, tile_block, precision=lax.Precision.HIGHEST)
        selector = ((targets[:, None] == block_ids[None, :]) & live_tiles[:, None]).astype(jnp.float32)
        summed = jnp.einsum("fti,tn->fni", products, selector, precision=lax.Precision.HIGHEST)
        return summed.reshape(F_IN, NP).astype(jnp.bfloat16)

    per_part = lax.map(one_part, jnp.arange(N_NODES, dtype=jnp.int32))
    aggregate = jnp.transpose(per_part, (1, 0, 2)).reshape(F_IN, NP * N_NODES)
    contract_first = (((0,), (0,)), ((), ()))
    contract_last = (((1,), (1,)), ((), ()))
    preact = lax.dot_general(w_self, features, contract_first, preferred_element_type=jnp.float32)
    preact = preact + lax.dot_general(w_neigh, aggregate, contract_first, preferred_element_type=jnp.float32)
    preact = preact + hidden_bias[:, None]
    sigmoid_value = jax.nn.sigmoid(preact)
    hidden = (preact * sigmoid_value).astype(jnp.bfloat16)
    pre_grad = (cotangent.astype(jnp.float32) * sigmoid_value * (1.0 + preact * (1.0 - sigmoid_value))).astype(jnp.bfloat16)
    grad_self = lax.dot_general(features, pre_grad, contract_last, preferred_element_type=jnp.float32)
    grad_neigh = lax.dot_general(aggregate, pre_grad, contract_last, preferred_element_type=jnp.float32)
    bias_grad = jnp.sum(pre_grad.astype(jnp.float32), axis=1)
    return hidden, grad_self, grad_neigh, bias_grad
```

```python
import functools

import jax
import jax.numpy as jnp
from jax import lax
from jax.experimental import pallas as pl
from jax.experimental.pallas import tpu as pltpu
from jax.sharding import PartitionSpec as P


LANES = 128
UNROLL = 4
VMEM = pltpu.MemorySpace.VMEM
SMEM = pltpu.MemorySpace.SMEM


def select_kernel(count_ref, features_ref, rows_ref, hub_ref, out_ref, wide_ref):
    width, nodes = features_ref.shape
    blocks = nodes // LANES
    parts = rows_ref.shape[0]
    hub_count = hub_ref.shape[1]
    groups = LANES // hub_count
    for block in range(blocks):
        wide_ref[block] = features_ref[:, block * LANES:(block + 1) * LANES].astype(jnp.float32)
    slots = lax.broadcasted_iota(jnp.int32, (width, LANES), 1)

    def picked(index, low, size):
        inside = index & (LANES - 1)
        home = index // LANES
        found = jnp.zeros((size, LANES), jnp.float32)
        for block in range(blocks):
            taken = jnp.take_along_axis(wide_ref[block, low:low + size], inside, axis=1)
            found = jnp.where(home == block, taken, found)
        return found

    hub_index = jnp.concatenate([hub_ref[...]] * groups, axis=1)
    rows = width // groups
    hub_index = jnp.broadcast_to(hub_index, (rows, LANES))
    packed = jnp.zeros((rows, LANES), jnp.float32)
    for group in range(groups):
        taken = picked(hub_index, group * rows, rows)
        packed = jnp.where(slots[:rows] // hub_count == group, taken, packed)
    packed = packed.astype(jnp.bfloat16)

    def one(part, carry):
        index = jnp.broadcast_to(rows_ref[part], (width, LANES))
        found = picked(index, 0, width)
        found = jnp.where(slots < count_ref[0, part], found, 0.0)
        out_ref[part, :width] = found.astype(jnp.bfloat16)
        out_ref[part, width:] = packed
        return carry

    lax.fori_loop(0, parts, one, 0)


def select(features, send_rows, send_count, hub_local):
    width, nodes = features.shape
    parts, slot_count = send_rows.shape[1:]
    rows = width * hub_local.shape[1] // LANES
    return pl.pallas_call(
        select_kernel,
        out_shape=jax.ShapeDtypeStruct((parts, width + rows, LANES), jnp.bfloat16),
        in_specs=[pl.BlockSpec(memory_space=SMEM)] + [pl.BlockSpec(memory_space=VMEM)] * 3,
        out_specs=pl.BlockSpec(memory_space=VMEM),
        scratch_shapes=[pltpu.VMEM((nodes // LANES, width, LANES), jnp.float32)],
        cost_estimate=pl.CostEstimate(flops=1000000, bytes_accessed=1000000, transcendentals=0),
        name="select",
    )(send_count, features, send_rows.reshape(parts, 1, slot_count), hub_local)


def main_kernel(
    pieces,
    hub_count,
    feat_ref,
    count_ref,
    target_ref,
    anchor_ref,
    *refs,
):
    own = refs[:pieces]
    halo = refs[pieces:2 * pieces]
    tiles_ref, weight_ref, bias_ref, cot_ref, hidden_ref, grad_ref, source_ref, acc_ref = refs[2 * pieces:]
    width, nodes = own[0].shape
    blocks = nodes // LANES
    parts = halo[0].shape[0]
    full = width * pieces
    hidden_width = weight_ref.shape[0]
    groups = LANES // hub_count
    rows = width // groups
    me = feat_ref[0]

    for k in range(pieces):
        base = pl.multiple_of((me ^ k) * width, width)
        for block in range(blocks):
            source_ref[block, pl.ds(base, width)] = own[k][:, block * LANES:(block + 1) * LANES]
        for part in range(parts):
            source_ref[blocks + part, pl.ds(base, width)] = halo[k][part, :width]
        lane_group = lax.broadcasted_iota(jnp.int32, (rows, LANES), 1) // hub_count
        for first in range(0, parts, groups):
            raw = [halo[k][first + j, width:].astype(jnp.float32) for j in range(groups)]
            made = []
            for group in range(groups):
                out = jnp.zeros((rows, LANES), jnp.float32)
                for j in range(groups):
                    moved = pltpu.roll(raw[j], ((j - group) % groups) * hub_count, 1)
                    out = jnp.where(lane_group == j, moved, out)
                made.append(out)
            source_ref[blocks + parts + first // groups, pl.ds(base, width)] = jnp.concatenate(
                made, axis=0
            ).astype(jnp.bfloat16)

    acc_ref[...] = jnp.zeros_like(acc_ref)
    live = count_ref[0]

    def step(turn, carry):
        made = []
        for u in range(UNROLL):
            t = turn * UNROLL + u
            alive = t < live
            anchor = jnp.where(alive, anchor_ref[0, t], 0)
            target = jnp.where(alive, target_ref[0, t], blocks)
            product = lax.dot_general(
                source_ref[anchor],
                tiles_ref[t],
                (((1,), (1,)), ((), ())),
                preferred_element_type=jnp.float32,
            )
            made.append((target, product))
        for target, product in made:
            acc_ref[target] += product
        return carry

    lax.fori_loop(0, (live + UNROLL - 1) // UNROLL, step, 0)

    weight = weight_ref[...]
    bias = bias_ref[...]
    ones = jnp.ones((8, LANES), jnp.bfloat16)

    def dense(block, carry):
        total, bias_total = carry
        both = jnp.concatenate([source_ref[block], acc_ref[block].astype(jnp.bfloat16)], axis=0)
        preact = jnp.dot(weight, both, preferred_element_type=jnp.float32) + bias
        gate = jax.nn.sigmoid(preact)
        here = pl.ds(pl.multiple_of(block * LANES, LANES), LANES)
        hidden_ref[:, here] = (preact * gate).astype(jnp.bfloat16)
        cot = cot_ref[:, here].astype(jnp.float32)
        pre_grad = (cot * gate * (1.0 + preact * (1.0 - gate))).astype(jnp.bfloat16)
        total = total + lax.dot_general(
            both, pre_grad, (((1,), (1,)), ((), ())), preferred_element_type=jnp.float32
        )
        bias_total = bias_total + lax.dot_general(
            ones, pre_grad, (((1,), (1,)), ((), ())), preferred_element_type=jnp.float32
        )
        return total, bias_total

    total, bias_total = lax.fori_loop(
        0,
        blocks,
        dense,
        (jnp.zeros((2 * full, hidden_width), jnp.float32), jnp.zeros((8, hidden_width), jnp.float32)),
    )
    grad_ref[:full] = jnp.concatenate([total[:full], total[full:]], axis=1)
    grad_ref[full:] = jnp.concatenate([bias_total, bias_total], axis=1)


def local(
    features,
    w_self,
    w_neigh,
    hidden_bias,
    cotangent,
    hub_local,
    send_rows,
    send_count,
    tile_values,
    tile_target,
    tile_anchor,
    tile_count,
):
    node_parts = lax.axis_size("nodes")
    feat_parts = lax.axis_size("feat")
    feat_index = lax.axis_index("feat")
    width_local, node_local = features.shape
    hub_count = hub_local.shape[1]
    hidden_local = w_self.shape[1] // feat_parts
    full = width_local * feat_parts
    blocks = node_local // LANES

    def feat_swap(value, bit):
        return lax.ppermute(value, "feat", [(i, i ^ bit) for i in range(feat_parts)])

    def node_swap(value, bit):
        return lax.ppermute(value, "nodes", [(i, i ^ bit) for i in range(node_parts)])

    def spread(value):
        held = [value]
        far = []
        bit = feat_parts // 2
        got = {0: value}
        while bit:
            for k in list(got):
                got[k ^ bit] = feat_swap(got[k], bit)
            bit //= 2
        return [got[k] for k in range(feat_parts)]

    outgoing = select(features, send_rows, send_count, hub_local)
    own = spread(features)
    incoming = lax.all_to_all(outgoing, "nodes", split_axis=0, concat_axis=0, tiled=True)
    halo = spread(incoming)

    self_cols = lax.dynamic_slice_in_dim(w_self, feat_index * hidden_local, hidden_local, 1)
    neigh_cols = lax.dynamic_slice_in_dim(w_neigh, feat_index * hidden_local, hidden_local, 1)
    weight = jnp.concatenate([self_cols, neigh_cols], axis=0).T
    bias = lax.dynamic_slice_in_dim(hidden_bias, feat_index * hidden_local, hidden_local, 0)[:, None]

    smem = pl.BlockSpec(memory_space=SMEM)
    vmem = pl.BlockSpec(memory_space=VMEM)
    source_blocks = blocks + node_parts + node_parts * hub_count // LANES
    hidden, grads = pl.pallas_call(
        functools.partial(main_kernel, feat_parts, hub_count),
        out_shape=(
            jax.ShapeDtypeStruct((hidden_local, node_local), jnp.bfloat16),
            jax.ShapeDtypeStruct((full + 8, 2 * hidden_local), jnp.float32),
        ),
        in_specs=[smem] * 4 + [vmem] * (2 * feat_parts + 4),
        out_specs=(vmem, vmem),
        scratch_shapes=[
            pltpu.VMEM((source_blocks, full, LANES), jnp.bfloat16),
            pltpu.VMEM((blocks + 1, full, LANES), jnp.float32),
        ],
        cost_estimate=pl.CostEstimate(flops=2000000000, bytes_accessed=6000000, transcendentals=300000),
        name="layer",
    )(
        feat_index.reshape(1).astype(jnp.int32),
        tile_count,
        tile_target,
        tile_anchor,
        *own,
        *halo,
        tile_values,
        weight,
        bias,
        cotangent,
    )
    bit = 1
    while bit < node_parts:
        grads = grads + node_swap(grads, bit)
        bit *= 2
    return (
        hidden,
        grads[:full, :hidden_local],
        grads[:full, hidden_local:],
        grads[full, :hidden_local],
    )


def solution(mesh):
    in_specs = (
        P("feat", "nodes"),
        P(),
        P(),
        P(),
        P("feat", "nodes"),
        P("nodes", None),
        P("nodes", None, None),
        P("nodes", None),
        P("nodes", None, None),
        P("nodes", None),
        P("nodes", None),
        P("nodes"),
    )
    out_specs = (P("feat", "nodes"), P(None, "feat"), P(None, "feat"), P("feat"))
    return jax.shard_map(local, mesh=mesh, in_specs=in_specs, out_specs=out_specs, check_vma=False)
```

```python
import functools

import jax
import jax.numpy as jnp
from jax import lax
from jax.experimental import pallas as pl
from jax.experimental.pallas import tpu as pltpu
from jax.sharding import PartitionSpec as P


LANES = 128
UNROLL = 4
CHUNK = 4
LIMIT = 24 * 1024 * 1024
VMEM = pltpu.MemorySpace.VMEM
SMEM = pltpu.MemorySpace.SMEM


def select_kernel(count_ref, features_ref, rows_ref, hub_ref, out_ref, wide_ref):
    width, nodes = features_ref.shape
    blocks = nodes // LANES
    parts = rows_ref.shape[0]
    hub_count = hub_ref.shape[1]
    groups = LANES // hub_count
    for block in range(blocks):
        wide_ref[block] = features_ref[:, block * LANES:(block + 1) * LANES].astype(jnp.float32)
    slots = lax.broadcasted_iota(jnp.int32, (width, LANES), 1)

    def picked(index, low, size):
        inside = index & (LANES - 1)
        home = index // LANES
        found = jnp.zeros((size, LANES), jnp.float32)
        for block in range(blocks):
            taken = jnp.take_along_axis(wide_ref[block, low:low + size], inside, axis=1)
            found = jnp.where(home == block, taken, found)
        return found

    hub_index = jnp.concatenate([hub_ref[...]] * groups, axis=1)
    rows = width // groups
    hub_index = jnp.broadcast_to(hub_index, (rows, LANES))
    packed = jnp.zeros((rows, LANES), jnp.float32)
    for group in range(groups):
        taken = picked(hub_index, group * rows, rows)
        packed = jnp.where(slots[:rows] // hub_count == group, taken, packed)
    packed = packed.astype(jnp.bfloat16)

    def one(part, carry):
        index = jnp.broadcast_to(rows_ref[part], (width, LANES))
        found = picked(index, 0, width)
        found = jnp.where(slots < count_ref[0, part], found, 0.0)
        out_ref[part, :width] = found.astype(jnp.bfloat16)
        out_ref[part, width:] = packed
        return carry

    lax.fori_loop(0, parts, one, 0)


def select(features, send_rows, send_count, hub_local):
    width, nodes = features.shape
    parts, slot_count = send_rows.shape[1:]
    rows = width * hub_local.shape[1] // LANES
    return pl.pallas_call(
        select_kernel,
        out_shape=jax.ShapeDtypeStruct((parts, width + rows, LANES), jnp.bfloat16),
        in_specs=[pl.BlockSpec(memory_space=SMEM)] + [pl.BlockSpec(memory_space=VMEM)] * 3,
        out_specs=pl.BlockSpec(memory_space=VMEM),
        scratch_shapes=[pltpu.VMEM((nodes // LANES, width, LANES), jnp.float32)],
        cost_estimate=pl.CostEstimate(flops=1000000, bytes_accessed=1000000, transcendentals=0),
        name="select",
    )(send_count, features, send_rows.reshape(parts, 1, slot_count), hub_local)


def own_kernel(
    pieces,
    feat_ref,
    count_ref,
    target_ref,
    anchor_ref,
    *refs,
):
    own = refs[:pieces]
    tiles_ref, self_ref, neigh_ref, bias_ref = refs[pieces:pieces + 4]
    acc_ref, source_ref, weight_ref, column_ref, plan_ref, list_ref, turn_ref = refs[pieces + 4:]
    width, nodes = own[0].shape
    blocks = nodes // LANES
    full = width * pieces
    hidden_width = weight_ref.shape[0]
    me = feat_ref[0]

    for k in range(pieces):
        base = pl.multiple_of((me ^ k) * width, width)
        for block in range(blocks):
            source_ref[block, pl.ds(base, width)] = own[k][:, block * LANES:(block + 1) * LANES]

    mine = pl.ds(pl.multiple_of(me * hidden_width, hidden_width), hidden_width)
    turn_ref[...] = self_ref[...].astype(jnp.float32).T
    weight_ref[:, :full] = turn_ref[mine].astype(jnp.bfloat16)
    turn_ref[...] = neigh_ref[...].astype(jnp.float32).T
    weight_ref[:, full:] = turn_ref[mine].astype(jnp.bfloat16)
    turn_ref[...] = jnp.broadcast_to(bias_ref[...], (LANES, bias_ref.shape[1])).T
    column_ref[...] = turn_ref[mine]

    acc_ref[...] = jnp.zeros_like(acc_ref)
    live = count_ref[0]

    def sort(t, counts):
        near, far = counts
        anchor = anchor_ref[0, t]
        target = target_ref[0, t]
        local = anchor < blocks

        @pl.when(local)
        def _():
            list_ref[0, near] = t
            list_ref[1, near] = target
            list_ref[2, near] = anchor

        @pl.when(jnp.logical_not(local))
        def _():
            plan_ref[0, far] = t
            plan_ref[1, far] = target
            plan_ref[2, far] = anchor - blocks

        return jnp.where(local, near + 1, near), jnp.where(local, far, far + 1)

    near, far = lax.fori_loop(0, live, sort, (0, 0))
    for u in range(UNROLL):
        list_ref[0, near + u] = 0
        list_ref[1, near + u] = blocks
        list_ref[2, near + u] = 0
        plan_ref[0, far + u] = 0
        plan_ref[1, far + u] = blocks
        plan_ref[2, far + u] = 0
    plan_ref[3, 0] = far
    run_tiles(near, list_ref, source_ref, tiles_ref, acc_ref)


def run_tiles(count, list_ref, source_ref, tiles_ref, acc_ref):
    def step(turn, carry):
        made = []
        for u in range(UNROLL):
            t = turn * UNROLL + u
            product = lax.dot_general(
                source_ref[list_ref[2, t]],
                tiles_ref[list_ref[0, t]],
                (((1,), (1,)), ((), ())),
                preferred_element_type=jnp.float32,
            )
            made.append((list_ref[1, t], product))
        for target, product in made:
            acc_ref[target] += product
        return carry

    lax.fori_loop(0, (count + UNROLL - 1) // UNROLL, step, 0)


def tail_kernel(
    pieces,
    hub_count,
    feat_ref,
    plan_ref,
    *refs,
):
    halo = refs[:pieces]
    near_ref, source_ref, tiles_ref, weight_ref, column_ref, cot_ref = refs[pieces:pieces + 6]
    hidden_ref, grad_ref, far_ref, acc_ref = refs[pieces + 6:]
    blocks, full = source_ref.shape[:2]
    width = full // pieces
    parts = halo[0].shape[0]
    hidden_width = weight_ref.shape[0]
    groups = LANES // hub_count
    rows = width // groups
    me = feat_ref[0]

    for k in range(pieces):
        base = pl.multiple_of((me ^ k) * width, width)
        for part in range(parts):
            far_ref[part, pl.ds(base, width)] = halo[k][part, :width]
        lane_group = lax.broadcasted_iota(jnp.int32, (rows, LANES), 1) // hub_count
        for first in range(0, parts, groups):
            raw = [halo[k][first + j, width:].astype(jnp.float32) for j in range(groups)]
            made = []
            for group in range(groups):
                out = jnp.zeros((rows, LANES), jnp.float32)
                for j in range(groups):
                    moved = pltpu.roll(raw[j], ((j - group) % groups) * hub_count, 1)
                    out = jnp.where(lane_group == j, moved, out)
                made.append(out)
            far_ref[parts + first // groups, pl.ds(base, width)] = jnp.concatenate(
                made, axis=0
            ).astype(jnp.bfloat16)

    acc_ref[...] = jnp.zeros_like(acc_ref)
    run_tiles(plan_ref[3, 0], plan_ref, far_ref, tiles_ref, acc_ref)

    weight = weight_ref[...]
    bias = jnp.concatenate([column_ref[...]] * CHUNK, axis=1)
    total = jnp.zeros((hidden_width, 2 * full), jnp.float32)
    bias_total = jnp.zeros((8, hidden_width), jnp.float32)
    ones = jnp.ones((8, CHUNK * LANES), jnp.bfloat16)
    for first in range(0, blocks, CHUNK):
        both = jnp.concatenate(
            [
                jnp.concatenate(
                    [source_ref[b], (near_ref[b] + acc_ref[b]).astype(jnp.bfloat16)], axis=0
                )
                for b in range(first, first + CHUNK)
            ],
            axis=1,
        )
        preact = jnp.dot(weight, both, preferred_element_type=jnp.float32) + bias
        gate = jax.nn.sigmoid(preact)
        here = slice(first * LANES, (first + CHUNK) * LANES)
        hidden_ref[:, here] = (preact * gate).astype(jnp.bfloat16)
        cot = cot_ref[:, here].astype(jnp.float32)
        pre_grad = (cot * gate * (1.0 + preact * (1.0 - gate))).astype(jnp.bfloat16)
        total = total + lax.dot_general(
            pre_grad, both, (((1,), (1,)), ((), ())), preferred_element_type=jnp.float32
        )
        bias_total = bias_total + lax.dot_general(
            ones, pre_grad, (((1,), (1,)), ((), ())), preferred_element_type=jnp.float32
        )
    grad_ref[:hidden_width] = total
    grad_ref[hidden_width:] = jnp.concatenate(
        [bias_total, jnp.zeros((8, 2 * full - hidden_width), jnp.float32)], axis=1
    )


def local(
    features,
    w_self,
    w_neigh,
    hidden_bias,
    cotangent,
    hub_local,
    send_rows,
    send_count,
    tile_values,
    tile_target,
    tile_anchor,
    tile_count,
):
    node_parts = lax.axis_size("nodes")
    feat_parts = lax.axis_size("feat")
    feat_index = lax.axis_index("feat")
    width_local, node_local = features.shape
    hub_count = hub_local.shape[1]
    hidden_local = w_self.shape[1] // feat_parts
    full = width_local * feat_parts
    blocks = node_local // LANES

    def feat_swap(value, bit):
        return lax.ppermute(value, "feat", [(i, i ^ bit) for i in range(feat_parts)])

    def node_swap(value, bit):
        return lax.ppermute(value, "nodes", [(i, i ^ bit) for i in range(node_parts)])

    def spread(value):
        held = [value]
        far = []
        bit = feat_parts // 2
        got = {0: value}
        while bit:
            for k in list(got):
                got[k ^ bit] = feat_swap(got[k], bit)
            bit //= 2
        return [got[k] for k in range(feat_parts)]

    outgoing = select(features, send_rows, send_count, hub_local)
    own = spread(features)
    incoming = lax.all_to_all(outgoing, "nodes", split_axis=0, concat_axis=0, tiled=True)
    halo = spread(incoming)

    smem = pl.BlockSpec(memory_space=SMEM)
    vmem = pl.BlockSpec(memory_space=VMEM)
    tile_slots = tile_values.shape[0]
    far_blocks = node_parts + node_parts * hub_count // LANES
    me = feat_index.reshape(1).astype(jnp.int32)
    near, source, weight, column, plan = pl.pallas_call(
        functools.partial(own_kernel, feat_parts),
        out_shape=(
            jax.ShapeDtypeStruct((blocks + 1, full, LANES), jnp.float32),
            jax.ShapeDtypeStruct((blocks, full, LANES), jnp.bfloat16),
            jax.ShapeDtypeStruct((hidden_local, 2 * full), jnp.bfloat16),
            jax.ShapeDtypeStruct((hidden_local, LANES), jnp.float32),
            jax.ShapeDtypeStruct((4, tile_slots + LANES), jnp.int32),
        ),
        in_specs=[smem] * 4 + [vmem] * (feat_parts + 4),
        out_specs=(vmem, vmem, vmem, vmem, smem),
        scratch_shapes=[
            pltpu.SMEM((4, tile_slots + LANES), jnp.int32),
            pltpu.VMEM((w_self.shape[1], full), jnp.float32),
        ],
        compiler_params=pltpu.CompilerParams(vmem_limit_bytes=LIMIT),
        cost_estimate=pl.CostEstimate(flops=2000000000, bytes_accessed=6000000, transcendentals=300000),
        name="own",
    )(
        me,
        tile_count,
        tile_target,
        tile_anchor,
        *own,
        tile_values,
        w_self,
        w_neigh,
        hidden_bias.reshape(1, -1),
    )
    hidden, grads = pl.pallas_call(
        functools.partial(tail_kernel, feat_parts, hub_count),
        out_shape=(
            jax.ShapeDtypeStruct((hidden_local, node_local), jnp.bfloat16),
            jax.ShapeDtypeStruct((hidden_local + 8, 2 * full), jnp.float32),
        ),
        in_specs=[smem] * 2 + [vmem] * (feat_parts + 6),
        out_specs=(vmem, vmem),
        scratch_shapes=[
            pltpu.VMEM((far_blocks, full, LANES), jnp.bfloat16),
            pltpu.VMEM((blocks + 1, full, LANES), jnp.float32),
        ],
        compiler_params=pltpu.CompilerParams(vmem_limit_bytes=LIMIT),
        cost_estimate=pl.CostEstimate(flops=2000000000, bytes_accessed=6000000, transcendentals=300000),
        name="tail",
    )(me, plan, *halo, near, source, tile_values, weight, column, cotangent)
    bit = 1
    while bit < node_parts:
        grads = grads + node_swap(grads, bit)
        bit *= 2
    return (
        hidden,
        grads[:hidden_local, :full].T,
        grads[:hidden_local, full:].T,
        grads[hidden_local, :hidden_local],
    )


def solution(mesh):
    in_specs = (
        P("feat", "nodes"),
        P(),
        P(),
        P(),
        P("feat", "nodes"),
        P("nodes", None),
        P("nodes", None, None),
        P("nodes", None),
        P("nodes", None, None),
        P("nodes", None),
        P("nodes", None),
        P("nodes"),
    )
    out_specs = (P("feat", "nodes"), P(None, "feat"), P(None, "feat"), P("feat"))
    return jax.shard_map(local, mesh=mesh, in_specs=in_specs, out_specs=out_specs, check_vma=False)
```
